32 devices in a mesh: frame: 8 (over z, x), rec: 4 (over y, core).
Axes of the slice: x: 2, y: 2, z: 4, core: 2. Of those that a mesh axis runs over, the one named last changes fastest.
Arguments:
- inputs: bfloat16 [4, 8192, 512], P('rec', 'frame'), may hold values from -6 to 6
- conv_weight: bfloat16 [5, 512, 512], replicated, may hold values from -4 to 4
- conv_bias: float32 [512], replicated, may hold values from -3 to 3
- labels: int32 [4, 8192, 512], P('rec', 'frame'), may hold values 0 or 1
- rec_span: int32 [2, 4, 8192], P(None, 'rec', 'frame'), may hold values from 0 to 1023, as said below
Outputs:
- features: bfloat16 [4, 8192, 512], P('rec', 'frame')
- probe_weights: float32 [512, 512], replicated
The draws below stay inside these ranges and needn't reach their ends.
Inputs may be any that keep to these rules, and one draw needn't show every extreme that they name: Each stream is a series of whole recordings of at most 1024 frames, the last one possibly cut by the stream's end: rec_span[0, g, t] counts the frames of t's recording before t and rec_span[1, g, t] those after t within the stream; in every stream some recording has exactly 1024 frames.
All inputs are finite; a program needn't handle non-finite values. No bound on the sum of `labels` on one device may be relied on, other than what follows from the above.
Results may differ from the reference program's by a relative error of at most 0.0035.
The reference program's roundings to bfloat16 on the way (of `joined`) count: a program that leaves them out, or rounds other values in their place, can miss the bound.
Values may be sent and summed in bfloat16 or wider, within the bound.
A program may use at most 64 MiB of HBM per device.

```python
import math
import jax
import jax.numpy as jnp
from jax import lax

CIN = 512
FEAT = 512
LABELS = 512
TAPS = 5
REC_MOST = 1024
REC_MIN = 64
TIME = 8192
GROUPS = 4
FRAMES = 32768


def draw_rec_span(key, part):
    record_count = TIME // REC_MIN + 1
    stream_keys = jax.random.split(key, GROUPS)

    def one_stream(stream_key):
        length_key, pick_key = jax.random.split(stream_key)
        lengths = jax.random.randint(length_key, (record_count,), REC_MIN, REC_MOST + 1).astype(jnp.int32)
        longest = jax.random.randint(pick_key, (), 0, max(TIME // REC_MOST - 1, 1)).astype(jnp.int32)
        lengths = jnp.where(jnp.arange(record_count, dtype=jnp.int32) == longest, REC_MOST, lengths).astype(jnp.int32)
        record_ends = jnp.cumsum(lengths).astype(jnp.int32)
        record_starts = record_ends - lengths
        position = jnp.arange(TIME, dtype=jnp.int32)
        record_index = jnp.searchsorted(record_ends, position, side='right').astype(jnp.int32)
        before = position - record_starts[record_index]
        frames_after = jnp.minimum(record_ends[record_index], TIME) - 1 - position
        return jnp.stack([before, frames_after]).astype(jnp.int32)
    stream_spans = jax.vmap(one_stream)(stream_keys)
    return jnp.transpose(stream_spans, (1, 0, 2)).astype(jnp.int32)


def draw_conv_weight(key, part):
    base_key = jax.random.fold_in(key, 11)
    delta_key = jax.random.fold_in(key, 12)
    spread_key = jax.random.fold_in(key, 13)
    order_key = jax.random.fold_in(key, 14)
    family_count = FEAT // 4
    base = jnp.clip(jax.random.normal(base_key, (TAPS, CIN, family_count), jnp.float32), -3.0, 3.0)
    delta = jnp.clip(jax.random.normal(delta_key, (TAPS, CIN, FEAT), jnp.float32), -3.0, 3.0)
    spread = jnp.exp(jax.random.uniform(spread_key, (FEAT,), jnp.float32, math.log(0.02), 0.0))
    family = (jax.random.permutation(order_key, FEAT).astype(jnp.int32) // 4).astype(jnp.int32)
    picked = jnp.take(base, family, axis=2)
    weight = 6.0 / math.sqrt(TAPS * CIN) * (picked + spread[None, None, :] * delta)
    return weight.astype(jnp.float32).astype(jnp.bfloat16)


def plant(drawn, key, smallest, top_value):
    longest = drawn.shape.index(max(drawn.shape))
    spots = []
    for shift in (0, 1):
        where = [jax.random.randint(jax.random.fold_in(key, axis), (), 0, length) for axis, length in enumerate(drawn.shape)]
        where[longest] = (where[longest] + shift) % drawn.shape[longest]
        spots.append(tuple(where))
    return drawn.at[spots[0]].set(smallest).at[spots[1]].set(top_value)


def block_levels(rng, shape, cuts, low, high):
    def one(dim, blocks):
        draws = jax.random.uniform(jax.random.fold_in(jax.random.fold_in(rng, 6), dim), (blocks,), jnp.float32, low / len(cuts), high / len(cuts))
        return jnp.repeat(jnp.exp(draws), shape[dim] // blocks).reshape((-1,) + (1,) * (len(shape) - dim - 1))

    level = one(*cuts[0])
    for cut in cuts[1:]:
        level = level * one(*cut)
    return level


def noise(rng, extent, deviation, reach, cuts=(), kind=jnp.bfloat16):
    array = deviation * jax.random.normal(rng, extent, jnp.float32)
    if cuts:
        array = array * block_levels(rng, extent, cuts, -0.22, 0.18)
    return jnp.clip(array, -reach, reach).astype(kind)


def setup_inputs(seed: int = 0) -> dict:
    keys = jax.random.split(jax.random.key(seed), 6)
    return {
        "inputs": noise(keys[0], (GROUPS, TIME, CIN), 1.0, 6.0, ((0, 4), (1, 8))),
        "conv_weight": draw_conv_weight(jax.random.fold_in(keys[5], 71), 0),
        "conv_bias": noise(keys[2], (FEAT,), 0.5, 3.0, (), jnp.float32),
        "labels": plant((jax.random.randint(keys[3], (GROUPS, TIME, LABELS), 0, 4) < 1).astype(jnp.int32), jax.random.fold_in(keys[3], 1), 0, 1),
        "rec_span": draw_rec_span(jax.random.fold_in(keys[5], 71), 0),
    }


RIDGE = 0.1

def stack_taps(stream, before, frames_after):
    half_width = TAPS // 2
    shard_rows = stream.shape[0]
    padded = jnp.pad(stream, ((half_width, half_width), (0, 0)))
    pieces = []
    for tap_index in range(TAPS):
        offset = tap_index - half_width
        shifted = padded[tap_index:tap_index + shard_rows]
        if offset < 0:
            keep_mask = before >= -offset
        elif offset > 0:
            keep_mask = frames_after >= offset
        else:
            keep_mask = before >= 0
        pieces.append(jnp.where(keep_mask[:, None], shifted, jnp.zeros_like(shifted)))
    return jnp.concatenate(pieces, axis=1)

def reference(inputs, conv_weight, conv_bias, labels, rec_span):
    flat_weight = conv_weight.reshape(TAPS * CIN, FEAT)

    def one_group(packed):
        stream, label_rows, before, frames_after = packed
        stacked = stack_taps(stream, before, frames_after)
        pre_act = jnp.dot(stacked.astype(jnp.float32), flat_weight.astype(jnp.float32), preferred_element_type=jnp.float32) + conv_bias
        group_feats = jax.nn.gelu(pre_act, approximate=False).astype(jnp.bfloat16)
        joined = jnp.concatenate([group_feats, label_rows.astype(jnp.bfloat16)], axis=1)
        moments = jnp.dot(group_feats.T.astype(jnp.float32), joined.astype(jnp.float32), preferred_element_type=jnp.float32)
        totals = lax.optimization_barrier(jnp.sum(joined.astype(jnp.float32), axis=0))
        return (group_feats, moments, totals)
    features, moments, totals = lax.map(one_group, (inputs, labels, rec_span[0], rec_span[1]))
    moments = lax.optimization_barrier(jnp.sum(moments, axis=0))
    totals = lax.optimization_barrier(jnp.sum(totals, axis=0))
    frame_count = jnp.float32(FRAMES)
    feat_totals = totals[:FEAT]
    label_totals = totals[FEAT:]
    covariance = (moments[:, :FEAT] - feat_totals[:, None] * feat_totals[None, :] / frame_count) / frame_count
    covariance = covariance + RIDGE * jnp.eye(FEAT, dtype=jnp.float32)
    cross_terms = (moments[:, FEAT:] - feat_totals[:, None] * label_totals[None, :] / frame_count) / jnp.sqrt(frame_count)
    factor = jnp.linalg.cholesky(covariance)
    probe_weights = jax.scipy.linalg.cho_solve((factor, True), cross_terms)
    return (features, probe_weights)
```

```python
import math
import jax
import jax.numpy as jnp
from jax import lax
from jax.experimental import pallas as pl
from jax.experimental.pallas import tpu as pltpu
from jax.sharding import PartitionSpec as P

RIDGE = 0.1
TILE = 128
HI = lax.Precision.HIGHEST
GROUP = 4

def mm(a, b):
    return jnp.dot(a, b, precision=HI, preferred_element_type=jnp.float32)

def mtm(a, b):
    return lax.dot_general(a, b, (((0,), (0,)), ((), ())), precision=HI, preferred_element_type=jnp.float32)

def invert_tile(slabs):
    count = len(slabs)
    width = 8 * count
    lane = lax.broadcasted_iota(jnp.int32, (8, width), 1)
    sub = lax.broadcasted_iota(jnp.int32, (8, width), 0)
    def spread(row):
        return jnp.broadcast_to(row, (8, width))
    for j in range(0, width, GROUP):
        home, base = j // 8, j % 8
        cols = [[jnp.broadcast_to(s[:, j + b:j + b + 1], (8, width)) for b in range(GROUP)] for s in slabs]
        piv = [[spread(cols[home][b][base + a:base + a + 1]) for b in range(GROUP)] for a in range(GROUP)]
        in_group = (lane >= j) & (lane < j + GROUP)
        rows = []
        for a in range(GROUP):
            row = spread(slabs[home][base + a:base + a + 1])
            rows.append(jnp.where(in_group, jnp.where(lane == j + a, 1.0, 0.0), row))
        for a in range(GROUP):
            inv = 1.0 / piv[a][a]
            rows[a] = rows[a] * inv
            for b in range(a + 1, GROUP):
                piv[a][b] = piv[a][b] * inv
            for o in range(GROUP):
                if o != a:
                    f = piv[o][a]
                    rows[o] = rows[o] - f * rows[a]
                    for b in range(a + 1, GROUP):
                        piv[o][b] = piv[o][b] - f * piv[a][b]
        fresh = []
        for i, s in enumerate(slabs):
            v = jnp.where(in_group, 0.0, s)
            for b in range(GROUP):
                v = v - cols[i][b] * rows[b]
            if i == home:
                for a in range(GROUP):
                    v = jnp.where(sub == base + a, rows[a], v)
            fresh.append(v)
        slabs = fresh
    return slabs

def factor(a_ref, inv_ref, w_ref, tile):
    size = a_ref.shape[0]
    n = size // tile
    def step(k, carry):
        at = pl.multiple_of(k * tile, tile)
        slabs = [a_ref[pl.ds(at + 8 * i, 8), pl.ds(at, tile)] for i in range(tile // 8)]
        for i, s in enumerate(invert_tile(slabs)):
            inv_ref[pl.ds(at + 8 * i, 8), :] = s
        for c in range(n - 1):
            @pl.when(k == c)
            def _():
                lo, hi = c * tile, (c + 1) * tile
                row = a_ref[lo:hi, hi:]
                w = mm(inv_ref[lo:hi, :], row)
                w_ref[lo:hi, hi:] = w
                for i in range(c + 1, n):
                    s = slice(i * tile, (i + 1) * tile)
                    a_ref[s, i * tile:] -= mtm(a_ref[lo:hi, s], w[:, (i - c - 1) * tile:])
        return carry
    lax.fori_loop(0, n, step, 0)

def substitute(a_ref, inv_ref, w_ref, x_ref, y_ref, tile):
    size = a_ref.shape[0]
    n = size // tile
    for k in range(n):
        lo, hi = k * tile, (k + 1) * tile
        if k:
            x = x_ref[lo:hi, :] - mtm(w_ref[:lo, lo:hi], y_ref[:lo, :])
        else:
            x = x_ref[lo:hi, :]
        y_ref[lo:hi, :] = x
    for k in reversed(range(n)):
        lo, hi = k * tile, (k + 1) * tile
        y = mm(inv_ref[lo:hi, :], y_ref[lo:hi, :])
        if k < n - 1:
            y = y - mm(w_ref[lo:hi, hi:], y_ref[hi:, :])
        y_ref[lo:hi, :] = y


def bits_of(axis, size):
    return [(axis, 1 << i) for i in range(size.bit_length() - 1)]


class Stream:
    def __init__(self, stages, src, out, inbox, sems):
        self.stages, self.src, self.out, self.inbox, self.sems = stages, src, out, inbox, sems
        self.lo, self.length, self.at, self.used = 0, out.shape[0], 0, 0
        self.held, self.copy = (src, 0), None

    def done(self):
        return self.at == 2 * len(self.stages)

    def start(self):
        count = len(self.stages)
        down = self.at < count
        axis, step = self.stages[self.at if down else 2 * count - 1 - self.at]
        me = lax.axis_index(axis)
        self.bit = lax.rem(me // step, 2)
        peer = me + (1 - 2 * self.bit) * step
        if down:
            half = self.length // 2
            ref, base = self.held
            src = ref.at[pl.ds(base + (1 - self.bit) * half, half)]
            dst = self.inbox.at[pl.ds(self.used, half)]
        else:
            src = dst = self.out.at[pl.ds(self.lo, self.length)]
        self.copy = pltpu.make_async_remote_copy(
            src_ref=src, dst_ref=dst,
            send_sem=self.sems.at[0, self.at], recv_sem=self.sems.at[1, self.at],
            device_id={axis: peer}, device_id_type=pl.DeviceIdType.MESH,
        )
        self.copy.start()

    def finish(self):
        self.copy.wait()
        if self.at < len(self.stages):
            half = self.length // 2
            ref, base = self.held
            total = ref[pl.ds(base + self.bit * half, half)] + self.inbox[pl.ds(self.used, half)]
            self.lo, self.length = self.lo + self.bit * half, half
            if self.at < len(self.stages) - 1:
                self.inbox[pl.ds(self.used, half)] = total
                self.held = (self.inbox, self.used)
            else:
                self.out[pl.ds(self.lo, half)] = total
            self.used += half
        else:
            self.lo, self.length = self.lo - self.bit * self.length, 2 * self.length
        self.at += 1


def greet(stages):
    barrier = pltpu.get_barrier_semaphore()
    for axis, step in stages:
        me = lax.axis_index(axis)
        peer = me + (1 - 2 * lax.rem(me // step, 2)) * step
        pl.semaphore_signal(barrier, inc=1, device_id={axis: peer}, device_id_type=pl.DeviceIdType.MESH)
    pl.semaphore_wait(barrier, len(stages))


def orders(frame_size, rec_size):
    frame, rec = bits_of("frame", frame_size), bits_of("rec", rec_size)
    return rec + frame, rec[:1] + frame + rec[1:]


def reduce_kernel(sizes, g_in, x_in, g_out, x_out, g_box, x_box, g_sem, x_sem):
    one, two = orders(*sizes)
    greet(one)
    streams = [Stream(one, g_in, g_out, g_box, g_sem), Stream(two, x_in, x_out, x_box, x_sem)]
    for s in streams:
        s.start()
    while not all(s.done() for s in streams):
        for s in streams:
            if not s.done():
                s.finish()
                if not s.done():
                    s.start()


def reduce_all(g, x):
    sizes = (lax.axis_size("frame"), lax.axis_size("rec"))
    count = len(orders(*sizes)[0])
    vmem = pl.BlockSpec(memory_space=pltpu.VMEM)
    return pl.pallas_call(
        lambda *refs: reduce_kernel(sizes, *refs),
        out_shape=[jax.ShapeDtypeStruct(v.shape, v.dtype) for v in (g, x)],
        in_specs=[vmem, vmem],
        out_specs=[vmem, vmem],
        scratch_shapes=[
            pltpu.VMEM(g.shape, jnp.float32),
            pltpu.VMEM(x.shape, jnp.float32),
            pltpu.SemaphoreType.DMA((2, 2 * count)),
            pltpu.SemaphoreType.DMA((2, 2 * count)),
        ],
        compiler_params=pltpu.CompilerParams(collective_id=0, has_side_effects=True),
    )(g, x)


def pairs(n):
    return [(i, j) for i in range(n) for j in range(i, n)]


def tile_at(ref, slot):
    units = TILE // 8
    return ref[slot * units:(slot + 1) * units].reshape(TILE, TILE)


def column(totals, i):
    return jnp.broadcast_to(totals[i:i + 1], (TILE, TILE)).T


def solve_kernel(frames, g_ref, x_ref, y_ref, a_ref, inv_ref, w_ref, c_ref):
    size, n = a_ref.shape[0], a_ref.shape[0] // TILE
    m = y_ref.shape[1] // TILE
    units = TILE // 8
    rows = -(-(n + m) // 8)
    first = len(pairs(n)) * units
    totals = g_ref[first:first + rows].reshape(8 * rows, TILE)
    cols = [column(totals, i) for i in range(n)]
    eye = lax.broadcasted_iota(jnp.int32, (TILE, TILE), 0) == lax.broadcasted_iota(jnp.int32, (TILE, TILE), 1)
    for slot, (i, j) in enumerate(pairs(n)):
        v = (tile_at(g_ref, slot) - cols[i] * totals[j:j + 1] / frames) / frames
        if i == j:
            v = v + jnp.where(eye, RIDGE, 0.0)
        a_ref[i * TILE:(i + 1) * TILE, j * TILE:(j + 1) * TILE] = v
    factor(a_ref, inv_ref, w_ref, TILE)
    for i in range(n):
        for j in range(m):
            v = tile_at(x_ref, i * m + j) - cols[i] * totals[n + j:n + j + 1] / frames
            c_ref[i * TILE:(i + 1) * TILE, j * TILE:(j + 1) * TILE] = v / math.sqrt(frames)
    substitute(a_ref, inv_ref, w_ref, c_ref, y_ref, TILE)


def solve(g, x, size, wide, frames):
    vmem = pl.BlockSpec(memory_space=pltpu.VMEM)
    return pl.pallas_call(
        lambda *refs: solve_kernel(frames, *refs),
        out_shape=jax.ShapeDtypeStruct((size, wide), jnp.float32),
        in_specs=[vmem, vmem],
        out_specs=vmem,
        scratch_shapes=[
            pltpu.VMEM((size, size), jnp.float32),
            pltpu.VMEM((size, TILE), jnp.float32),
            pltpu.VMEM((size, size), jnp.float32),
            pltpu.VMEM((size, wide), jnp.float32),
        ],
    )(g, x)


def pad_units(v, devices):
    extra = -v.shape[0] % devices
    return jnp.pad(v, ((0, extra), (0, 0), (0, 0)))


def padded_2(shard, sides, width):
    for axis, dim in sides:
        size, length = (lax.axis_size(axis), shard.shape[dim])
        up = [(i, (i + 1) % size) for i in range(size - 1)]
        down = [(j, i) for i, j in up]
        last = lax.slice_in_dim(shard, length - width, length, axis=dim)
        leading = lax.slice_in_dim(shard, 0, width, axis=dim)
        before = lax.ppermute(last, axis, up)
        after = lax.ppermute(leading, axis, down)
        shard = jnp.concatenate([before, shard, after], axis=dim)
    return shard


def per_device(inputs, conv_weight, conv_bias, labels, rec_span):
    tap_count = conv_weight.shape[0]
    half_width = tap_count // 2
    shard_rows = inputs.shape[1]
    feat_width = conv_weight.shape[2]
    padded = padded_2(inputs, (("frame", 1),), half_width)
    before = rec_span[0, 0]
    frames_after = rec_span[1, 0]
    pieces = []
    for tap_index in range(tap_count):
        offset = tap_index - half_width
        shifted = padded[0, tap_index : tap_index + shard_rows]
        if offset < 0:
            keep_mask = before >= -offset
        elif offset > 0:
            keep_mask = frames_after >= offset
        else:
            keep_mask = before >= 0
        pieces.append(jnp.where(keep_mask[:, None], shifted, jnp.zeros_like(shifted)))
    stacked = jnp.concatenate(pieces, axis=1)
    flat_weight = conv_weight.reshape(tap_count * conv_weight.shape[1], feat_width)
    pre_act = jnp.dot(stacked, flat_weight, preferred_element_type=jnp.float32) + conv_bias
    features = jax.nn.gelu(pre_act, approximate=False).astype(jnp.bfloat16)
    joined = jnp.concatenate([features, labels[0].astype(jnp.bfloat16)], axis=1)
    moments = lax.dot_general(
        features, joined, (((0,), (0,)), ((), ())), preferred_element_type=jnp.float32
    )
    totals = jnp.sum(joined, axis=0, dtype=jnp.float32)
    devices = lax.axis_size("frame") * lax.axis_size("rec")
    frames = float(shard_rows * devices)
    wide = labels.shape[2]
    n, m = feat_width // TILE, wide // TILE
    blocks = moments.reshape(n, TILE, n + m, TILE).transpose(0, 2, 1, 3)
    gram = jnp.concatenate([blocks[i, i:n].reshape(-1, 8, TILE) for i in range(n)])
    sums = totals.reshape(n + m, TILE)
    sums = jnp.pad(sums, ((0, -(n + m) % 8), (0, 0))).reshape(-1, 8, TILE)
    g = pad_units(jnp.concatenate([gram, sums]), devices)
    x = pad_units(blocks[:, n:].reshape(-1, 8, TILE), devices)
    g, x = reduce_all(g, x)
    return (features[None], solve(g, x, feat_width, wide, frames))


def solution(mesh):
    in_specs = (P("rec", "frame", None), P(), P(), P("rec", "frame", None), P(None, "rec", "frame"))
    out_specs = (P("rec", "frame", None), P())
    return jax.shard_map(
        per_device, mesh=mesh, in_specs=in_specs, out_specs=out_specs, check_vma=False
    )
```

```python
import math
import jax
import jax.numpy as jnp
from jax import lax
from jax.experimental import pallas as pl
from jax.experimental.pallas import tpu as pltpu
from jax.sharding import PartitionSpec as P

RIDGE = 0.1
TILE = 128
POINTS = 4
HI = lax.Precision.HIGHEST
GROUP = 4

def mm(a, b):
    return jnp.dot(a, b, precision=HI, preferred_element_type=jnp.float32)

def mtm(a, b):
    return lax.dot_general(a, b, (((0,), (0,)), ((), ())), precision=HI, preferred_element_type=jnp.float32)

def invert_tile(slabs, hook):
    count = len(slabs)
    width = 8 * count
    lane = lax.broadcasted_iota(jnp.int32, (8, width), 1)
    sub = lax.broadcasted_iota(jnp.int32, (8, width), 0)
    def spread(row):
        return jnp.broadcast_to(row, (8, width))
    for j in range(0, width, GROUP):
        home, base = j // 8, j % 8
        cols = [[jnp.broadcast_to(s[:, j + b:j + b + 1], (8, width)) for b in range(GROUP)] for s in slabs]
        piv = [[spread(cols[home][b][base + a:base + a + 1]) for b in range(GROUP)] for a in range(GROUP)]
        in_group = (lane >= j) & (lane < j + GROUP)
        rows = []
        for a in range(GROUP):
            row = spread(slabs[home][base + a:base + a + 1])
            rows.append(jnp.where(in_group, jnp.where(lane == j + a, 1.0, 0.0), row))
        for a in range(GROUP):
            inv = 1.0 / piv[a][a]
            rows[a] = rows[a] * inv
            for b in range(a + 1, GROUP):
                piv[a][b] = piv[a][b] * inv
            for o in range(GROUP):
                if o != a:
                    f = piv[o][a]
                    rows[o] = rows[o] - f * rows[a]
                    for b in range(a + 1, GROUP):
                        piv[o][b] = piv[o][b] - f * piv[a][b]
        fresh = []
        for i, s in enumerate(slabs):
            v = jnp.where(in_group, 0.0, s)
            for b in range(GROUP):
                v = v - cols[i][b] * rows[b]
            if i == home:
                for a in range(GROUP):
                    v = jnp.where(sub == base + a, rows[a], v)
            fresh.append(v)
        slabs = fresh
        if (j + GROUP) * POINTS % width == 0:
            hook((j + GROUP) * POINTS // width - 1)
    return slabs

def factor(a_ref, inv_ref, w_ref, tile, hook):
    size = a_ref.shape[0]
    n = size // tile
    def step(k, carry):
        at = pl.multiple_of(k * tile, tile)
        slabs = [a_ref[pl.ds(at + 8 * i, 8), pl.ds(at, tile)] for i in range(tile // 8)]
        for i, s in enumerate(invert_tile(slabs, lambda p: hook(k, p))):
            inv_ref[pl.ds(at + 8 * i, 8), :] = s
        for c in range(n - 1):
            @pl.when(k == c)
            def _():
                lo, hi = c * tile, (c + 1) * tile
                row = a_ref[lo:hi, hi:]
                w = mm(inv_ref[lo:hi, :], row)
                w_ref[lo:hi, hi:] = w
                for i in range(c + 1, n):
                    s = slice(i * tile, (i + 1) * tile)
                    a_ref[s, i * tile:] -= mtm(a_ref[lo:hi, s], w[:, (i - c - 1) * tile:])
        return carry
    lax.fori_loop(0, n, step, 0)

def substitute(a_ref, inv_ref, w_ref, x_ref, y_ref, tile):
    size = a_ref.shape[0]
    n = size // tile
    for k in range(n):
        lo, hi = k * tile, (k + 1) * tile
        if k:
            x = x_ref[lo:hi, :] - mtm(w_ref[:lo, lo:hi], y_ref[:lo, :])
        else:
            x = x_ref[lo:hi, :]
        y_ref[lo:hi, :] = x
    for k in reversed(range(n)):
        lo, hi = k * tile, (k + 1) * tile
        y = mm(inv_ref[lo:hi, :], y_ref[lo:hi, :])
        if k < n - 1:
            y = y - mm(w_ref[lo:hi, hi:], y_ref[hi:, :])
        y_ref[lo:hi, :] = y


def bits_of(axis, size):
    return [(axis, 1 << i) for i in range(size.bit_length() - 1)]


class Stream:
    def __init__(self, stages, src, out, inbox, sems):
        self.sems, self.plan = sems, []
        ref, base, lo, length, used = src, 0, 0, out.shape[0], 0
        bits = []
        for at, (axis, step) in enumerate(stages):
            me = lax.axis_index(axis)
            bit = lax.rem(me // step, 2)
            bits.append(bit)
            half = length // 2
            where = {axis: me + (1 - 2 * bit) * step}
            send = (ref, base + (1 - bit) * half, inbox, used, half, where)
            lo = lo + bit * half
            last = at == len(stages) - 1
            into = (out, lo) if last else (inbox, used)
            self.plan.append((send, (ref, base + bit * half, inbox, used, half) + into))
            ref, base, length = inbox, used, half
            used += half
        for (axis, step), bit in reversed(list(zip(stages, bits))):
            me = lax.axis_index(axis)
            where = {axis: me + (1 - 2 * bit) * step}
            self.plan.append(((out, lo, out, lo, length, where), None))
            lo, length = lo - bit * length, 2 * length

    def copy(self, at):
        src, s, dst, d, size, where = self.plan[at][0]
        return pltpu.make_async_remote_copy(
            src_ref=src.at[pl.ds(s, size)], dst_ref=dst.at[pl.ds(d, size)],
            send_sem=self.sems.at[0, at], recv_sem=self.sems.at[1, at],
            device_id=where, device_id_type=pl.DeviceIdType.MESH,
        )

    def start(self, at):
        if at < len(self.plan):
            self.copy(at).start()

    def finish(self, at):
        self.copy(at).wait()
        add = self.plan[at][1]
        if add is not None:
            ref, r, box, b, size, out, o = add
            out[pl.ds(o, size)] = ref[pl.ds(r, size)] + box[pl.ds(b, size)]


def greet(stages):
    barrier = pltpu.get_barrier_semaphore()
    for axis, step in stages:
        me = lax.axis_index(axis)
        peer = me + (1 - 2 * lax.rem(me // step, 2)) * step
        pl.semaphore_signal(barrier, inc=1, device_id={axis: peer}, device_id_type=pl.DeviceIdType.MESH)
    pl.semaphore_wait(barrier, len(stages))


def orders(frame_size, rec_size):
    frame, rec = bits_of("frame", frame_size), bits_of("rec", rec_size)
    return rec + frame, rec[:1] + frame + rec[1:]


def pairs(n):
    return [(i, j) for i in range(n) for j in range(i, n)]


def tile_at(ref, slot):
    units = TILE // 8
    return ref[slot * units:(slot + 1) * units].reshape(TILE, TILE)


def column(totals, i):
    return jnp.broadcast_to(totals[i:i + 1], (TILE, TILE)).T


def timetable(x, spots):
    total = x.plan[0][0][4]
    costs = [1 + 8 * send[4] / total for send, _ in x.plan[1:]]
    table, spent = {}, 0.0
    for at, cost in enumerate(costs[:-1], 1):
        spent += cost
        spot = min(spots - 1, math.ceil(spent / sum(costs) * spots) - 1)
        table.setdefault(spot, []).append(at)
    return table


def fused_kernel(sizes, frames, g_in, x_in, y_ref, g_ref, x_ref, g_box, x_box, a_ref, inv_ref, w_ref, c_ref, g_sem, x_sem):
    one, two = orders(*sizes)
    greet(one)
    g = Stream(one, g_in, g_ref, g_box, g_sem)
    x = Stream(two, x_in, x_ref, x_box, x_sem)
    g.start(0)
    for at in range(len(g.plan)):
        g.finish(at)
        g.start(at + 1)
        if at == 0:
            x.start(0)
    x.finish(0)
    x.start(1)
    size, n = a_ref.shape[0], a_ref.shape[0] // TILE
    m = y_ref.shape[1] // TILE
    units = TILE // 8
    rows = -(-(n + m) // 8)
    first = len(pairs(n)) * units
    totals = g_ref[first:first + rows].reshape(8 * rows, TILE)
    cols = [column(totals, i) for i in range(n)]
    eye = lax.broadcasted_iota(jnp.int32, (TILE, TILE), 0) == lax.broadcasted_iota(jnp.int32, (TILE, TILE), 1)
    for slot, (i, j) in enumerate(pairs(n)):
        v = (tile_at(g_ref, slot) - cols[i] * totals[j:j + 1] / frames) / frames
        if i == j:
            v = v + jnp.where(eye, RIDGE, 0.0)
        a_ref[i * TILE:(i + 1) * TILE, j * TILE:(j + 1) * TILE] = v
    table = timetable(x, n * POINTS)

    def hook(k, point):
        for c in range(n):
            stages = table.get(c * POINTS + point, [])
            if stages:
                @pl.when(k == c)
                def _():
                    for at in stages:
                        x.finish(at)
                        x.start(at + 1)

    factor(a_ref, inv_ref, w_ref, TILE, hook)
    x.finish(len(x.plan) - 1)
    totals = g_ref[first:first + rows].reshape(8 * rows, TILE)
    for i in range(n):
        col = column(totals, i)
        for j in range(m):
            v = tile_at(x_ref, i * m + j) - col * totals[n + j:n + j + 1] / frames
            c_ref[i * TILE:(i + 1) * TILE, j * TILE:(j + 1) * TILE] = v / math.sqrt(frames)
    substitute(a_ref, inv_ref, w_ref, c_ref, y_ref, TILE)


def reduce_and_solve(g, x, size, wide, frames):
    sizes = (lax.axis_size("frame"), lax.axis_size("rec"))
    count = len(orders(*sizes)[0])
    vmem = pl.BlockSpec(memory_space=pltpu.VMEM)
    return pl.pallas_call(
        lambda *refs: fused_kernel(sizes, frames, *refs),
        out_shape=jax.ShapeDtypeStruct((size, wide), jnp.float32),
        in_specs=[vmem, vmem],
        out_specs=vmem,
        scratch_shapes=[
            pltpu.VMEM(g.shape, jnp.float32),
            pltpu.VMEM(x.shape, jnp.float32),
            pltpu.VMEM(g.shape, jnp.float32),
            pltpu.VMEM(x.shape, jnp.float32),
            pltpu.VMEM((size, size), jnp.float32),
            pltpu.VMEM((size, TILE), jnp.float32),
            pltpu.VMEM((size, size), jnp.float32),
            pltpu.VMEM((size, wide), jnp.float32),
            pltpu.SemaphoreType.DMA((2, 2 * count)),
            pltpu.SemaphoreType.DMA((2, 2 * count)),
        ],
        compiler_params=pltpu.CompilerParams(collective_id=0, has_side_effects=True),
    )(g, x)


def pad_units(v, devices):
    extra = -v.shape[0] % devices
    return jnp.pad(v, ((0, extra), (0, 0), (0, 0)))


def padded_2(shard, sides, width):
    for axis, dim in sides:
        size, length = (lax.axis_size(axis), shard.shape[dim])
        up = [(i, (i + 1) % size) for i in range(size - 1)]
        down = [(j, i) for i, j in up]
        last = lax.slice_in_dim(shard, length - width, length, axis=dim)
        leading = lax.slice_in_dim(shard, 0, width, axis=dim)
        before = lax.ppermute(last, axis, up)
        after = lax.ppermute(leading, axis, down)
        shard = jnp.concatenate([before, shard, after], axis=dim)
    return shard


def per_device(inputs, conv_weight, conv_bias, labels, rec_span):
    tap_count = conv_weight.shape[0]
    half_width = tap_count // 2
    shard_rows = inputs.shape[1]
    feat_width = conv_weight.shape[2]
    padded = padded_2(inputs, (("frame", 1),), half_width)
    before = rec_span[0, 0]
    frames_after = rec_span[1, 0]
    pieces = []
    for tap_index in range(tap_count):
        offset = tap_index - half_width
        shifted = padded[0, tap_index : tap_index + shard_rows]
        if offset < 0:
            keep_mask = before >= -offset
        elif offset > 0:
            keep_mask = frames_after >= offset
        else:
            keep_mask = before >= 0
        pieces.append(jnp.where(keep_mask[:, None], shifted, jnp.zeros_like(shifted)))
    stacked = jnp.concatenate(pieces, axis=1)
    flat_weight = conv_weight.reshape(tap_count * conv_weight.shape[1], feat_width)
    pre_act = jnp.dot(stacked, flat_weight, preferred_element_type=jnp.float32) + conv_bias
    features = jax.nn.gelu(pre_act, approximate=False).astype(jnp.bfloat16)
    joined = jnp.concatenate([features, labels[0].astype(jnp.bfloat16)], axis=1)
    moments = lax.dot_general(
        features, joined, (((0,), (0,)), ((), ())), preferred_element_type=jnp.float32
    )
    totals = jnp.sum(joined, axis=0, dtype=jnp.float32)
    devices = lax.axis_size("frame") * lax.axis_size("rec")
    frames = float(shard_rows * devices)
    wide = labels.shape[2]
    n, m = feat_width // TILE, wide // TILE
    blocks = moments.reshape(n, TILE, n + m, TILE).transpose(0, 2, 1, 3)
    gram = jnp.concatenate([blocks[i, i:n].reshape(-1, 8, TILE) for i in range(n)])
    sums = totals.reshape(n + m, TILE)
    sums = jnp.pad(sums, ((0, -(n + m) % 8), (0, 0))).reshape(-1, 8, TILE)
    g = pad_units(jnp.concatenate([gram, sums]), devices)
    x = pad_units(blocks[:, n:].reshape(-1, 8, TILE), devices)
    return (features[None], reduce_and_solve(g, x, feat_width, wide, frames))


def solution(mesh):
    in_specs = (P("rec", "frame", None), P(), P(), P("rec", "frame", None), P(None, "rec", "frame"))
    out_specs = (P("rec", "frame", None), P())
    return jax.shard_map(
        per_device, mesh=mesh, in_specs=in_specs, out_specs=out_specs, check_vma=False
    )
```
